32 devices in a mesh: dom: 8 (over y, x, core), rep: 4 (over z).
Axes of the slice: x: 2, y: 2, z: 4, core: 2. Of those that a mesh axis runs over, the one named last changes fastest.
Arguments:
- entities: float32 [8, 512, 400], P('dom', 'rep'), may hold values from -6 to 6
- entity_state: float32 [8, 512], P('dom', 'rep'), may hold values from 1e-08 to 0.01
- relations: float32 [768, 400], replicated, may hold values from -0.3125 to 0.3125
- relation_state: float32 [768], replicated, may hold values from 100 to 10000
- lhs_rows: int32 [8, 2048], P('dom', 'rep'), may hold values from 0 to 127
- rhs_rows: int32 [8, 2048], P('dom', 'rep'), may hold values from 0 to 127
- relation_ids: int32 [8, 2048], P('dom', 'rep'), may hold values from 0 to 767
- neg_rows: int32 [8, 16, 1000], P('dom', 'rep'), may hold values from 0 to 127
- matching: int32 [8], replicated, may hold values from 0 to 7, each once
- edge_counts: int32 [8, 4], P('dom', 'rep'), may hold values from 64 to 512, as said below
Outputs:
- new_entities: float32 [8, 512, 400], P('dom', 'rep')
- new_entity_state: float32 [8, 512], P('dom', 'rep')
- new_relations: float32 [768, 400], replicated
- new_relation_state: float32 [768], replicated
The draws below stay inside these ranges and needn't reach their ends.
Inputs may be any that keep to these rules, and one draw needn't show every extreme that they name: `edge_counts`: every device has at least 64 live edge slots, and some device has all 512. `matching`: each partition is the partner of exactly one partition.
All inputs are finite; a program needn't handle non-finite values.
Results may differ from the reference program's by a relative error of at most 0.0021.
Values may be sent and summed in bfloat16 or wider, within the bound.
No kernel may reach another device: no remote copies, remote signals or barrier semaphores. Data moves between devices by JAX's collectives and lax.ppermute only.
A program may use at most 64 MiB of HBM per device.

```python
import math
import jax
import jax.numpy as jnp
import numpy as np
from jax import lax

D = 400
NREL = 768
NEG = 1000
BLOCK = 128
EDGES_DEV = 512
ROWS_DEV = 128
BLOCKS_DEV = 4
PART_ROWS = 512
N_DOM = 8
N_REP = 4


def draw_edge_counts(key, part):
    base_key, spot_key = jax.random.split(jax.random.fold_in(key, 11))
    base_counts = jax.random.randint(base_key, (N_DOM, N_REP), EDGES_DEV // 8, EDGES_DEV // 2 + 1)
    spot = jax.random.randint(spot_key, (), 0, N_DOM * N_REP)
    flat_index = jnp.arange(N_DOM * N_REP, dtype=jnp.int32).reshape(N_DOM, N_REP)
    return jnp.where(flat_index == spot, EDGES_DEV, base_counts).astype(jnp.int32)


def draw_entity_state(key, part):
    lowest = math.log(1e-08)
    highest = math.log(0.01)
    exponent = jax.random.uniform(jax.random.fold_in(key, 23), (N_DOM, PART_ROWS), jnp.float32, lowest, highest)
    return jnp.clip(jnp.exp(exponent), 1e-08, 0.01).astype(jnp.float32)


def with_ends(array, stream_key, smallest, largest):
    longest = array.shape.index(max(array.shape))
    spots = []
    for shift in (0, 1):
        where = [jax.random.randint(jax.random.fold_in(stream_key, axis), (), 0, length) for axis, length in enumerate(array.shape)]
        where[longest] = (where[longest] + shift) % array.shape[longest]
        spots.append(tuple(where))
    return array.at[spots[0]].set(smallest).at[spots[1]].set(largest)


def level_of(stream_key, shape, cuts, smallest, largest):
    gain = 1.0
    for position, parts in cuts:
        draws = jax.random.uniform(jax.random.fold_in(jax.random.fold_in(stream_key, 6), position), (parts,), jnp.float32, smallest / len(cuts), largest / len(cuts))
        gain = gain * jnp.repeat(jnp.exp(draws), shape[position] // parts).reshape((-1,) + (1,) * (len(shape) - 1 - position))
    return gain


def rank_bounds(count, lean):
    weights = [(1 << 20) // math.isqrt(grade ** lean) + 1 for grade in range(1, count + 1)]
    deviation = 1 + sum(weights) // (1 << 30)
    return np.cumsum(np.array([max(1, weight // deviation) for weight in weights]))


def ranked(key, dims, amount, skew):
    table = rank_bounds(amount, skew)
    lot = jax.random.randint(jax.random.fold_in(key, 1), dims, 0, int(table[amount - 1]))
    grade = jnp.searchsorted(jnp.asarray(table, jnp.int32), lot, side="right")
    return jax.random.permutation(jax.random.fold_in(key, 2), amount)[grade].astype(jnp.int32)


def noise(own_key, shape, deviation, reach, shards=(), kind=jnp.bfloat16):
    drawn = jax.random.normal(own_key, shape, jnp.float32) * deviation
    if len(shards) > 0:
        drawn = level_of(own_key, shape, shards, -0.22, 0.18) * drawn
    return jnp.clip(drawn, min=-reach, max=reach).astype(kind)


def setup_inputs(seed: int = 0) -> dict:
    key_of = jax.random.split(jax.random.key(seed), 11)
    entities = noise(key_of[0], (N_DOM, PART_ROWS, D), 1.0, 6.0, ((0, 8), (1, 4)), jnp.float32)
    entity_state = draw_entity_state(jax.random.fold_in(key_of[10], 71), 0)
    relations = noise(key_of[2], (NREL, D), D ** -0.5, 0.3125, (), jnp.float32)
    relation_state = jnp.clip(jnp.exp(jax.random.uniform(key_of[3], (NREL,), jnp.float32, math.log(100.0), math.log(10000.0))), 100.0, 10000.0)
    lhs_rows = with_ends(jax.random.randint(key_of[4], (N_DOM, EDGES_DEV * N_REP), 0, ROWS_DEV), jax.random.fold_in(key_of[4], 1), 0, ROWS_DEV - 1).astype(jnp.int32)
    rhs_rows = with_ends(jax.random.randint(key_of[5], (N_DOM, EDGES_DEV * N_REP), 0, ROWS_DEV), jax.random.fold_in(key_of[5], 1), 0, ROWS_DEV - 1).astype(jnp.int32)
    relation_ids = with_ends(ranked(key_of[6], (N_DOM, EDGES_DEV * N_REP), NREL, 2), jax.random.fold_in(key_of[6], 3), 0, NREL - 1).astype(jnp.int32)
    neg_rows = with_ends(jax.random.randint(key_of[7], (N_DOM, BLOCKS_DEV * N_REP, NEG), 0, ROWS_DEV), jax.random.fold_in(key_of[7], 1), 0, ROWS_DEV - 1).astype(jnp.int32)
    matching = jax.random.permutation(key_of[8], N_DOM).astype(jnp.int32)
    edge_counts = draw_edge_counts(jax.random.fold_in(key_of[10], 71), 0)
    return {"entities": entities, "entity_state": entity_state, "relations": relations, "relation_state": relation_state, "lhs_rows": lhs_rows, "rhs_rows": rhs_rows, "relation_ids": relation_ids, "neg_rows": neg_rows, "matching": matching, "edge_counts": edge_counts}


LEARN = 0.1
EPSILON = 1e-06

def segment_bounds(feat_width):
    return (0, feat_width // 8, feat_width // 4, feat_width // 2, feat_width)

def block_grads(own_bf, partner_bf, relations, lhs_block, rhs_block, rel_block, neg_block, live_mask):
    feat_width = relations.shape[1]
    left_rows = jnp.take(own_bf, lhs_block, axis=0).astype(jnp.float32)
    rel_rows = jnp.take(relations, rel_block, axis=0)
    lhs_rel = (left_rows * rel_rows).astype(jnp.bfloat16)
    right_rows = jnp.take(partner_bf, rhs_block, axis=0)
    negative_rows = jnp.take(partner_bf, neg_block, axis=0)
    neg_total = negative_rows.shape[0]
    bounds_list = segment_bounds(feat_width)
    pos_terms = lhs_rel.astype(jnp.float32) * right_rows.astype(jnp.float32)
    pos_scores = []
    neg_scores = []
    for segment in range(4):
        low_dim = bounds_list[segment]
        high_dim = bounds_list[segment + 1]
        pos_piece = lax.optimization_barrier(jnp.sum(pos_terms[:, low_dim:high_dim], axis=1))
        neg_piece = lax.dot_general(lhs_rel[:, low_dim:high_dim], negative_rows[:, low_dim:high_dim], (((1,), (1,)), ((), ())), preferred_element_type=jnp.float32)
        if segment:
            pos_piece = pos_scores[-1] + pos_piece
            neg_piece = neg_scores[-1] + neg_piece
        pos_scores.append(pos_piece)
        neg_scores.append(neg_piece)
    pos_coef = [-live_mask * jax.nn.sigmoid(-score) for score in pos_scores]
    neg_coef = [live_mask[:, None] * jax.nn.sigmoid(score) / neg_total for score in neg_scores]
    pos_weight = [None] * 4
    neg_weight = [None] * 4
    pos_run = pos_coef[3]
    neg_run = neg_coef[3]
    pos_weight[3] = pos_run
    neg_weight[3] = neg_run.astype(jnp.bfloat16)
    for segment in (2, 1, 0):
        pos_run = pos_run + pos_coef[segment]
        neg_run = neg_run + neg_coef[segment]
        pos_weight[segment] = pos_run
        neg_weight[segment] = neg_run.astype(jnp.bfloat16)
    grad_lhs_parts = []
    grad_right_parts = []
    grad_neg_parts = []
    for segment in range(4):
        low_dim = bounds_list[segment]
        high_dim = bounds_list[segment + 1]
        lhs_piece = lhs_rel[:, low_dim:high_dim]
        neg_piece = negative_rows[:, low_dim:high_dim]
        grad_lhs_parts.append(pos_weight[segment][:, None] * right_rows[:, low_dim:high_dim].astype(jnp.float32) + jnp.dot(neg_weight[segment], neg_piece, preferred_element_type=jnp.float32))
        grad_right_parts.append(pos_weight[segment][:, None] * lhs_piece.astype(jnp.float32))
        grad_neg_parts.append(lax.dot_general(neg_weight[segment], lhs_piece, (((0,), (0,)), ((), ())), preferred_element_type=jnp.float32))
    grad_lhs_rel = jnp.concatenate(grad_lhs_parts, axis=1)
    grad_right = jnp.concatenate(grad_right_parts, axis=1)
    grad_negative = jnp.concatenate(grad_neg_parts, axis=1)
    return (grad_lhs_rel * rel_rows, grad_right, grad_negative, grad_lhs_rel * left_rows)

def device_grads(own_bf, partner_bf, relations, lhs_slots, rhs_slots, rel_slots, neg_slots, live_count, blocks_used):

    def visit_block(block_no, totals):
        grad_own, grad_partner, grad_rel = totals
        block_index = jnp.asarray(block_no, jnp.int32)
        first_edge = block_index * BLOCK
        lhs_block = lax.dynamic_slice_in_dim(lhs_slots, first_edge, BLOCK)
        rhs_block = lax.dynamic_slice_in_dim(rhs_slots, first_edge, BLOCK)
        rel_block = lax.dynamic_slice_in_dim(rel_slots, first_edge, BLOCK)
        neg_block = lax.dynamic_index_in_dim(neg_slots, block_index, 0, keepdims=False)
        live_mask = (first_edge + jnp.arange(BLOCK, dtype=jnp.int32) < live_count).astype(jnp.float32)
        grad_left, grad_right, grad_negative, grad_relrow = block_grads(own_bf, partner_bf, relations, lhs_block, rhs_block, rel_block, neg_block, live_mask)
        grad_own = grad_own.at[lhs_block].add(grad_left)
        grad_partner = grad_partner.at[rhs_block].add(grad_right).at[neg_block].add(grad_negative)
        grad_rel = grad_rel.at[rel_block].add(grad_relrow)
        return (grad_own, grad_partner, grad_rel)
    start_totals = (jnp.zeros(own_bf.shape, jnp.float32), jnp.zeros(partner_bf.shape, jnp.float32), jnp.zeros(relations.shape, jnp.float32))
    return lax.fori_loop(0, blocks_used, visit_block, start_totals)

def adagrad(values, state, gradient):
    new_state = state + lax.optimization_barrier(jnp.mean(gradient * gradient, axis=-1))
    return (values - LEARN * gradient / (jnp.sqrt(new_state)[..., None] + EPSILON), new_state)

def add_slice(entity_grads, part_no, row_start, anchor, addition):
    current = lax.dynamic_slice(entity_grads, (part_no, row_start, anchor), (1, ROWS_DEV, D))
    return lax.dynamic_update_slice(entity_grads, current + addition[None], (part_no, row_start, anchor))

def reference(entities, entity_state, relations, relation_state, lhs_rows, rhs_rows, relation_ids, neg_rows, matching, edge_counts):
    embed_bf = entities.astype(jnp.bfloat16)
    anchor = jnp.zeros((), jnp.int32)

    def visit(totals, device_no):
        entity_grads, relation_grad = totals
        part_no = (device_no // N_REP).astype(jnp.int32)
        slot_no = (device_no % N_REP).astype(jnp.int32)
        partner_no = matching[part_no].astype(jnp.int32)
        row_start = slot_no * ROWS_DEV
        edge_start = slot_no * EDGES_DEV
        own_bf = lax.dynamic_slice(embed_bf, (part_no, row_start, anchor), (1, ROWS_DEV, D))[0]
        partner_bf = lax.dynamic_slice(embed_bf, (partner_no, row_start, anchor), (1, ROWS_DEV, D))[0]
        lhs_slots = lax.dynamic_slice(lhs_rows, (part_no, edge_start), (1, EDGES_DEV))[0]
        rhs_slots = lax.dynamic_slice(rhs_rows, (part_no, edge_start), (1, EDGES_DEV))[0]
        rel_slots = lax.dynamic_slice(relation_ids, (part_no, edge_start), (1, EDGES_DEV))[0]
        neg_slots = lax.dynamic_slice(neg_rows, (part_no, slot_no * BLOCKS_DEV, anchor), (1, BLOCKS_DEV, NEG))[0]
        live_count = lax.dynamic_slice(edge_counts, (part_no, slot_no), (1, 1))[0, 0]
        grad_own, grad_partner, grad_rel = device_grads(own_bf, partner_bf, relations, lhs_slots, rhs_slots, rel_slots, neg_slots, live_count, BLOCKS_DEV)
        entity_grads = add_slice(entity_grads, part_no, row_start, anchor, grad_own)
        entity_grads = add_slice(entity_grads, partner_no, row_start, anchor, grad_partner)
        return ((entity_grads, relation_grad + grad_rel), None)
    start_totals = (jnp.zeros(entities.shape, jnp.float32), jnp.zeros(relations.shape, jnp.float32))
    (entity_grads, relation_grad), _ = lax.scan(visit, start_totals, jnp.arange(N_DOM * N_REP, dtype=jnp.int32))
    new_entities, new_entity_state = adagrad(entities, entity_state, entity_grads)
    new_relations, new_relation_state = adagrad(relations, relation_state, relation_grad)
    return (new_entities, new_entity_state, new_relations, new_relation_state)
```

```python
import functools

import jax
import jax.numpy as jnp
from jax import lax
from jax.experimental import pallas as pl
from jax.experimental.pallas import tpu as pltpu
from jax.sharding import PartitionSpec as P

BLOCK = 128
LANES = 128
LEARN = 0.1
EPSILON = 1e-06
F32 = jnp.float32
BF16 = jnp.bfloat16


def segment_bounds(feat_width):
    return (0, feat_width // 8, feat_width // 4, feat_width // 2, feat_width)


def split_bf(value):
    high = value.astype(BF16)
    return high, (value - high.astype(F32)).astype(BF16)


def dot_nn(a, b):
    return lax.dot_general(a, b, (((1,), (0,)), ((), ())), preferred_element_type=F32)


def dot_nt(a, b):
    return lax.dot_general(a, b, (((1,), (1,)), ((), ())), preferred_element_type=F32)


def dot_tn(a, b):
    return lax.dot_general(a, b, (((0,), (0,)), ((), ())), preferred_element_type=F32)


def one_hot_t(ids_row, first, count):
    rows = lax.broadcasted_iota(jnp.int32, (count, ids_row.shape[1]), 0) + first
    return jnp.where(rows == ids_row, 1.0, 0.0).astype(BF16)


def prep_kernel(ids_ref, neg_ref, own_ref, rel_ref, left_ref, relrow_ref, lhs_ref, count_ref):
    slice_rows = own_ref.shape[0]
    rel_total = rel_ref.shape[0]
    neg_total = neg_ref.shape[1]
    ids = ids_ref[...]
    left_hot = one_hot_t(ids[0:1], 0, slice_rows)
    left = dot_tn(left_hot, own_ref[...].astype(BF16))
    left_ref[...] = left.astype(BF16)
    rel_hot = one_hot_t(ids[2:3], 0, rel_total)
    rel_high, rel_low = split_bf(rel_ref[...])
    rel_rows = dot_tn(rel_hot, rel_high) + dot_tn(rel_hot, rel_low)
    relrow_ref[...] = rel_rows
    lhs_ref[...] = (left * rel_rows).astype(BF16)
    ones = jnp.ones((8, neg_total), BF16)
    for block in range(neg_ref.shape[0]):
        hot = one_hot_t(neg_ref[block : block + 1, :], 0, slice_rows)
        count_ref[block] = dot_nt(ones, hot)


def main_kernel(
    scal_ref,
    ids_ref,
    partner_ref,
    left_ref,
    relrow_ref,
    lhs_ref,
    count_ref,
    own_out,
    partner_out,
    keep_out,
    send_out,
    hot_ref,
    *,
    neg_total,
    rel_blocks,
    part_blocks,
):
    edges, feat = lhs_ref.shape
    rows = partner_ref.shape[0]
    blocks = edges // BLOCK
    bounds = segment_bounds(feat)
    near = min(feat, -(-bounds[3] // LANES) * LANES)
    live = scal_ref[0]
    ids = ids_ref[...]
    partner = partner_ref[...]
    lane = lax.broadcasted_iota(jnp.int32, (rows, feat), 1)
    zero = jnp.zeros((), BF16)
    prefix = jnp.concatenate(
        [jnp.where(lane[:, :near] < bounds[k + 1], partner[:, :near], zero) for k in range(3)], axis=0
    )
    within = [
        jnp.where((lane >= bounds[k]) & (lane < bounds[k + 1]), partner, zero) for k in range(4)
    ]
    within_near = jnp.concatenate([w[:, :near] for w in within], axis=0)
    within_far = within[3][:, near:]
    ids_col = jnp.transpose(ids)
    row_iota = lax.broadcasted_iota(jnp.int32, (BLOCK, rows), 1)
    edge_iota = lax.broadcasted_iota(jnp.int32, (BLOCK, rows), 0)
    lane_mask = lax.broadcasted_iota(jnp.int32, (rows, feat), 1)
    grad_partner_near = [None] * 4
    grad_partner_far = None
    left_parts = []
    rel_parts = []
    for block in range(blocks):
        span = slice(block * BLOCK, (block + 1) * BLOCK)
        lhs = lhs_ref[span, :]
        scores = dot_nt(lhs[:, :near], prefix)
        score_list = [scores[:, k * rows : (k + 1) * rows] for k in range(3)] + [dot_nt(lhs, partner)]
        alive = (edge_iota + block * BLOCK) < live
        weight = jnp.where(alive, count_ref[block][0:1, :] * (1.0 / neg_total), 0.0)
        hit = (row_iota == ids_col[span, 1:2]) & alive
        run = None
        weights = [None] * 4
        for k in (3, 2, 1, 0):
            score = score_list[k]
            tail = jnp.exp(-jnp.abs(score))
            big = 1.0 / (1.0 + tail)
            small = tail * big
            up = score >= 0.0
            coef = weight * jnp.where(up, big, small) - jnp.where(hit, jnp.where(up, small, big), 0.0)
            run = coef if run is None else run + coef
            weights[k] = split_bf(run)
        high = jnp.concatenate([w[0] for w in weights], axis=1)
        low = jnp.concatenate([w[1] for w in weights], axis=1)
        grad_near = dot_nn(high, within_near) + dot_nn(low, within_near)
        grad_far = dot_nn(weights[3][0], within_far) + dot_nn(weights[3][1], within_far)
        grad = jnp.concatenate([grad_near, grad_far], axis=1)
        left_parts.append(grad * relrow_ref[span, :])
        rel_parts.append(grad * left_ref[span, :].astype(F32))
        for k in range(4):
            part = dot_tn(weights[k][0], lhs[:, :near]) + dot_tn(weights[k][1], lhs[:, :near])
            grad_partner_near[k] = part if block == 0 else grad_partner_near[k] + part
        part = dot_tn(weights[3][0], lhs[:, near:]) + dot_tn(weights[3][1], lhs[:, near:])
        grad_partner_far = part if block == 0 else grad_partner_far + part
    lane_near = lane_mask[:, :near]
    gathered = grad_partner_near[3]
    for k in (2, 1, 0):
        gathered = jnp.where(lane_near < bounds[k + 1], grad_partner_near[k], gathered)
    grad_partner = jnp.concatenate([gathered, grad_partner_far], axis=1).astype(BF16)
    piece = rows // part_blocks
    for k in range(part_blocks):
        start = pl.multiple_of(scal_ref[1 + rel_blocks + k], piece)
        partner_out[pl.ds(start, piece), :] = grad_partner[k * piece : (k + 1) * piece, :]
    left_high, left_low = split_bf(jnp.concatenate(left_parts, axis=0))
    left_hot = one_hot_t(ids[0:1], 0, own_out.shape[0])
    own_out[...] = dot_nn(left_hot, left_high) + dot_nn(left_hot, left_low)
    rel_high, rel_low = split_bf(jnp.concatenate(rel_parts, axis=0))
    rel_piece = hot_ref.shape[0] // rel_blocks
    for k in range(rel_blocks):
        hot_ref[k * rel_piece : (k + 1) * rel_piece, :] = one_hot_t(ids[2:3], scal_ref[1 + k], rel_piece)
    kept = keep_out.shape[0]
    hot = hot_ref[...]
    grad_rel = dot_nn(hot, rel_high) + dot_nn(hot, rel_low)
    keep_out[...] = grad_rel[:kept]
    send_out[...] = grad_rel[kept:].astype(send_out.dtype)


def vmem_specs(count):
    return [pl.BlockSpec(memory_space=pltpu.VMEM) for _ in range(count)]


def smem_spec():
    return pl.BlockSpec(memory_space=pltpu.SMEM)


def prepare(ids, negatives, own_rows, relations):
    edges = ids.shape[1]
    slice_rows, feat = own_rows.shape
    return pl.pallas_call(
        prep_kernel,
        in_specs=vmem_specs(4),
        out_specs=vmem_specs(4),
        out_shape=(
            jax.ShapeDtypeStruct((edges, feat), BF16),
            jax.ShapeDtypeStruct((edges, feat), F32),
            jax.ShapeDtypeStruct((edges, feat), BF16),
            jax.ShapeDtypeStruct((negatives.shape[0], 8, slice_rows), F32),
        ),
        name="prep",
    )(ids, negatives, own_rows, relations)


def train(scalars, ids, partner, left, rel_rows, lhs, counts, *, rel_total, neg_total, rel_blocks, part_blocks, rel_out):
    edges, feat = lhs.shape
    rows = partner.shape[0]
    kept, sent, sent_type = rel_out
    return pl.pallas_call(
        functools.partial(
            main_kernel, neg_total=neg_total, rel_blocks=rel_blocks, part_blocks=part_blocks
        ),
        in_specs=[smem_spec()] + vmem_specs(6),
        out_specs=vmem_specs(4),
        out_shape=(
            jax.ShapeDtypeStruct((rows, feat), F32),
            jax.ShapeDtypeStruct((rows, feat), BF16),
            jax.ShapeDtypeStruct((kept, feat), F32),
            jax.ShapeDtypeStruct((sent, feat), sent_type),
        ),
        scratch_shapes=[pltpu.VMEM((rel_total, edges), BF16)],
        name="train",
    )(scalars, ids, partner, left, rel_rows, lhs, counts)


def finish_kernel(
    scal_ref,
    rel_ref,
    rel_state_ref,
    ent_ref,
    ent_state_ref,
    own_grad_ref,
    ent_own_ref,
    mine_ref,
    mine1_ref,
    mine2_ref,
    mine3_ref,
    peer_ref,
    peer1_ref,
    peer2_ref,
    peer3_ref,
    ent_out,
    ent_state_out,
    rel_out,
    rel_state_out,
    grad_ref,
    ent_grad_ref,
):
    piece = mine_ref.shape[0]
    quarter = ent_own_ref.shape[0]
    feat = rel_ref.shape[1]
    mine = (mine_ref, mine1_ref, mine2_ref, mine3_ref)
    peer = (peer_ref, peer1_ref, peer2_ref, peer3_ref)
    for s in range(4):
        start = pl.multiple_of(scal_ref[s], piece)
        grad_ref[pl.ds(start, piece), :] = mine[s][0:piece, :]
        start = pl.multiple_of(scal_ref[4 + s], piece)
        grad_ref[pl.ds(start, piece), :] = peer[s][0:piece, :]
        start = pl.multiple_of(scal_ref[8 + s], quarter)
        part = ent_own_ref[...] if s == 0 else mine[s][piece : piece + quarter, :]
        ent_grad_ref[pl.ds(start, quarter), :] = part
    adagrad_rows(rel_ref, rel_state_ref, grad_ref[...].astype(F32), rel_out, rel_state_out)
    adagrad_rows(ent_ref, ent_state_ref, own_grad_ref[...] + ent_grad_ref[...].astype(F32), ent_out, ent_state_out)


def adagrad_rows(values_ref, state_ref, grad, values_out, state_out):
    feat = grad.shape[1]
    mean = jnp.sum(grad * grad, axis=1, keepdims=True) * (1.0 / feat)
    for part in range(grad.shape[0] // LANES):
        span = slice(part * LANES, (part + 1) * LANES)
        state_row = jnp.broadcast_to(state_ref[0:1, span], (LANES, LANES))
        new_state = jnp.transpose(state_row) + jnp.broadcast_to(mean[span], (LANES, LANES))
        state_out[0:1, span] = jnp.transpose(new_state)[0:1, :]
        scale = LEARN / (jnp.sqrt(new_state[:, 0:1]) + EPSILON)
        values_out[span, :] = values_ref[span, :] - grad[span] * scale


def finish(scalars, relations, rel_state, entities, ent_state, own_grad, ent_own, mine, peer):
    rel_total, feat = relations.shape
    rows = entities.shape[0]
    outs = pl.pallas_call(
        finish_kernel,
        in_specs=[smem_spec()] + vmem_specs(14),
        out_specs=vmem_specs(4),
        out_shape=(
            jax.ShapeDtypeStruct((rows, feat), F32),
            jax.ShapeDtypeStruct((1, rows), F32),
            jax.ShapeDtypeStruct((rel_total, feat), F32),
            jax.ShapeDtypeStruct((1, rel_total), F32),
        ),
        scratch_shapes=[pltpu.VMEM((rel_total, feat), BF16), pltpu.VMEM((rows, feat), BF16)],
        name="finish",
    )(scalars, relations, rel_state, entities, ent_state, own_grad, ent_own, *mine, *peer)
    return outs


def adagrad(values, state, gradient):
    new_state = state + jnp.mean(gradient * gradient, axis=-1)
    return (values - LEARN * gradient / (jnp.sqrt(new_state)[..., None] + EPSILON), new_state)


def fetch_partner(own_bf, matching):
    peer_count = lax.axis_size("dom")
    slice_rows, feat_width = own_bf.shape
    pieces = own_bf.reshape(peer_count, slice_rows // peer_count, feat_width)
    spread = lax.all_to_all(pieces, "dom", split_axis=0, concat_axis=0, tiled=True)
    ordered = jnp.take(spread, matching, axis=0)
    arrived = lax.all_to_all(ordered, "dom", split_axis=0, concat_axis=0, tiled=True)
    return arrived.reshape(slice_rows, feat_width)


def invert(matching):
    positions = jnp.arange(matching.shape[0], dtype=jnp.int32)
    return jnp.sum(jnp.where(matching[None, :] == positions[:, None], positions[None, :], 0), axis=1)


def wide_step(own_rows, ent_state, relations, rel_state, ids, negatives, matching, live):
    prepared = prepare(ids, negatives, own_rows, relations)
    partner = fetch_partner(own_rows.astype(BF16), matching)
    rel_total = relations.shape[0]
    rows = own_rows.shape[0]
    half = rel_total // 2
    scalars = jnp.concatenate(
        [live[None], jnp.arange(2, dtype=jnp.int32) * half, jnp.zeros((1,), jnp.int32)]
    )
    grad_own, grad_partner, rel_low, rel_high = train(
        scalars, ids, partner, *prepared, rel_total=rel_total, neg_total=negatives.shape[1],
        rel_blocks=2, part_blocks=1, rel_out=(half, half, F32),
    )
    returned = fetch_partner(grad_partner, invert(matching)).astype(F32)
    new_rows, new_row_state = adagrad(own_rows, ent_state, grad_own + returned)
    total = lax.psum(jnp.concatenate([rel_low, rel_high], axis=0), ("dom", "rep"))
    new_relations, new_rel_state = adagrad(relations, rel_state, total)
    return new_rows, new_row_state, new_relations, new_rel_state


def swap(value, axis, shift):
    size = lax.axis_size(axis)
    return lax.ppermute(value, axis, [(i, i ^ shift) for i in range(size)])


def pick(index, choices):
    out = choices[-1]
    for number in range(len(choices) - 1):
        out = jnp.where(index == number, choices[number], out)
    return out


def near_step(own_rows, ent_state, relations, rel_state, ids, negatives, matching, live):
    rel_total, feat = relations.shape
    rows = own_rows.shape[0]
    half = rel_total // 2
    piece = half // 4
    quarter = rows // 4
    place = lax.axis_index("dom")
    core = place & 1
    chip = place >> 1
    shifts = jnp.arange(4, dtype=jnp.int32)

    own_bf = own_rows.astype(BF16)
    near = [own_bf] + [swap(own_bf, "dom", 2 * s) for s in (1, 2, 3)]
    prepared = prepare(ids, negatives, own_rows, relations)
    wanted = matching[place]
    peer_wanted = matching[place ^ 1]
    crossed = swap(pick((peer_wanted >> 1) ^ chip, near), "dom", 1)
    partner = jnp.where((wanted & 1) == core, pick((wanted >> 1) ^ chip, near), crossed)

    own_bases = core * half + (shifts ^ chip) * piece
    peer_bases = (1 - core) * half + (shifts ^ chip) * piece
    scalars = jnp.concatenate([live[None], own_bases, peer_bases, (shifts ^ chip) * quarter])
    grad_own, grad_partner, keep, send = train(
        scalars, ids, partner, *prepared, rel_total=rel_total, neg_total=negatives.shape[1],
        rel_blocks=8, part_blocks=4, rel_out=(half, half, BF16),
    )
    chip_sum = keep + swap(send, "dom", 1).astype(F32)
    sends = [
        jnp.concatenate(
            [chip_sum[s * piece : (s + 1) * piece].astype(BF16), grad_partner[s * quarter : (s + 1) * quarter]]
        )
        for s in range(4)
    ]
    got = [swap(sends[s], "dom", 2 * s) for s in (1, 2, 3)]
    plane_sum = (
        chip_sum[:piece] + got[0][:piece].astype(F32) + got[1][:piece].astype(F32) + got[2][:piece].astype(F32)
    ).astype(BF16)
    mine = jnp.stack([grad_partner[:quarter]] + [g[piece:] for g in got])
    theirs = swap(mine, "dom", 1)
    layers = [plane_sum] + [swap(plane_sum, "rep", s) for s in (1, 2, 3)]
    layers = [value.astype(F32) for value in layers]
    total = ((layers[0] + layers[1]) + (layers[2] + layers[3])).astype(BF16)

    source = invert(matching)[2 * (chip ^ shifts) + core]
    both = jnp.concatenate([mine, theirs], axis=0)
    order = ((source >> 1) ^ chip) + jnp.where((source & 1) == core, 0, 4)
    routed = jnp.take(both, order, axis=0)
    outs = [swap(jnp.concatenate([total, routed[s]]), "dom", 2 * s) for s in (1, 2, 3)]
    mine_rel = [total] + outs
    peer_rel = [swap(value, "dom", 1) for value in mine_rel]
    scalars = jnp.concatenate([own_bases, peer_bases, (shifts ^ chip) * quarter])
    new_rows, new_row_state, new_relations, new_rel_state = finish(
        scalars, relations, rel_state[None], own_rows, ent_state[None], grad_own, routed[0], mine_rel, peer_rel
    )
    return new_rows, new_row_state[0], new_relations, new_rel_state[0]


def shards(
    entities,
    entity_state,
    relations,
    relation_state,
    lhs_rows,
    rhs_rows,
    relation_ids,
    neg_rows,
    matching,
    edge_counts,
):
    ids = jnp.concatenate(
        [lhs_rows, rhs_rows, relation_ids, jnp.zeros((5, lhs_rows.shape[1]), jnp.int32)], axis=0
    )
    small = lax.axis_size("dom") == 8 and lax.axis_size("rep") == 4
    step = near_step if small else wide_step
    new_rows, new_row_state, new_relations, new_rel_state = step(
        entities[0], entity_state[0], relations, relation_state, ids, neg_rows[0], matching, edge_counts[0, 0]
    )
    return (new_rows[None], new_row_state[None], new_relations, new_rel_state)


def solution(mesh):
    return jax.shard_map(
        shards,
        mesh=mesh,
        in_specs=(
            P("dom", "rep", None),
            P("dom", "rep"),
            P(),
            P(),
            P("dom", "rep"),
            P("dom", "rep"),
            P("dom", "rep"),
            P("dom", "rep", None),
            P(),
            P("dom", "rep"),
        ),
        out_specs=(P("dom", "rep", None), P("dom", "rep"), P(), P()),
        check_vma=False,
    )
```

```python
import functools

import jax
import jax.numpy as jnp
from jax import lax
from jax.experimental import pallas as pl
from jax.experimental.pallas import tpu as pltpu
from jax.sharding import PartitionSpec as P

BLOCK = 128
TILE = 16
LEARN = 0.1
EPSILON = 1e-06
F32 = jnp.float32
BF16 = jnp.bfloat16
VMEM_BYTES = 24 * 1024 * 1024


def segment_bounds(feat_width):
    return (0, feat_width // 8, feat_width // 4, feat_width // 2, feat_width)


def tile_up(value, tile):
    return -(-value // tile) * tile


def piece_rows(feat_width):
    step = (feat_width // 4) // TILE * TILE
    return step, feat_width - 3 * step


def split_bf(value):
    high = value.astype(BF16)
    return high, (value - high.astype(F32)).astype(BF16)


def dot_nn(a, b):
    return lax.dot_general(a, b, (((1,), (0,)), ((), ())), preferred_element_type=F32)


def dot_nt(a, b):
    return lax.dot_general(a, b, (((1,), (1,)), ((), ())), preferred_element_type=F32)


def one_hot(ids_row, count):
    rows = lax.broadcasted_iota(jnp.int32, (count, ids_row.shape[1]), 0)
    return jnp.where(rows == ids_row, 1.0, 0.0).astype(BF16)


def prep_kernel(lhs_ids, rel_ids, negatives, own, rel, left_out, relrow_out, lhs_out, count_out, left_hot, rel_hot):
    slice_rows = own.shape[1]
    hot = one_hot(lhs_ids[...], slice_rows)
    left_hot[...] = hot
    left = dot_nn(own[...].astype(BF16), hot)
    left_out[...] = left.astype(BF16)
    hot = one_hot(rel_ids[...], rel.shape[1])
    rel_hot[...] = hot
    rel_high, rel_low = split_bf(rel[...])
    rel_rows = dot_nn(rel_high, hot) + dot_nn(rel_low, hot)
    relrow_out[...] = rel_rows
    lhs_out[...] = (left * rel_rows).astype(BF16)
    ones = jnp.ones((BLOCK, negatives.shape[1]), BF16)
    for block in range(negatives.shape[0]):
        count_out[block] = dot_nt(one_hot(negatives[block : block + 1, :], slice_rows), ones)


def place_of(scal):
    core = scal[0] & 1
    return core, scal[0] >> 1


def choose(index, refs):
    out = refs[-1][...]
    for number in range(len(refs) - 1):
        out = jnp.where(index == number, refs[number][...], out)
    return out


def train_kernel(*refs, neg_total, candidates):
    scal, rhs_ids, left, rel_rows, lhs_ref, counts, left_hot, rel_hot = refs[:8]
    near = refs[8 : 8 + candidates]
    own_out, partner_out, keep_out, send_out = refs[8 + candidates :]
    feat, edges = lhs_ref.shape
    rows = near[0].shape[1]
    blocks = edges // BLOCK
    bounds = segment_bounds(feat)
    split = min(feat, tile_up(bounds[3], TILE))
    deep = min(feat, tile_up(bounds[3], 256))
    live = scal[1]
    core, chip = place_of(scal)
    if candidates > 1:
        wanted = scal[2 + scal[0]]
        local = choose((wanted >> 1) ^ chip, near[:-1])
        partner_t = jnp.where((wanted & 1) == core, local, near[-1][...])
    else:
        partner_t = near[0][...]
    zero = jnp.zeros((), BF16)
    partner = jnp.transpose(partner_t.astype(F32)).astype(BF16)
    lane = lax.broadcasted_iota(jnp.int32, (rows, deep), 1)
    prefix = jnp.concatenate(
        [jnp.where(lane < bounds[k + 1], partner[:, :deep], zero) for k in range(3)], axis=0
    )
    lhs = lhs_ref[...]
    scores_low = dot_nn(prefix, lhs[:deep])
    scores_all = dot_nn(partner, lhs)
    row_iota = lax.broadcasted_iota(jnp.int32, (rows, BLOCK), 0)
    edge_iota = lax.broadcasted_iota(jnp.int32, (rows, BLOCK), 1)
    high_parts = [[], [], [], []]
    low_parts = [[], [], [], []]
    for block in range(blocks):
        span = slice(block * BLOCK, (block + 1) * BLOCK)
        alive = (edge_iota + block * BLOCK) < live
        weight = jnp.where(alive, counts[block] * (1.0 / neg_total), 0.0)
        hit = (row_iota == rhs_ids[:, span]) & alive
        run = None
        for k in (3, 2, 1, 0):
            score = scores_all[:, span] if k == 3 else scores_low[k * rows : (k + 1) * rows, span]
            tail = jnp.exp(-jnp.abs(score))
            big = 1.0 / (1.0 + tail)
            small = tail * big
            up = score >= 0.0
            coef = weight * jnp.where(up, big, small) - jnp.where(hit, jnp.where(up, small, big), 0.0)
            run = coef if run is None else run + coef
            high, low = split_bf(run)
            high_parts[k].append(high)
            low_parts[k].append(low)
    high = jnp.concatenate([jnp.concatenate(p, axis=1) for p in high_parts], axis=0)
    low = jnp.concatenate([jnp.concatenate(p, axis=1) for p in low_parts], axis=0)
    sub = lax.broadcasted_iota(jnp.int32, (split, rows), 0)
    within = jnp.concatenate(
        [jnp.where((sub >= bounds[k]) & (sub < bounds[k + 1]), partner_t[:split], zero) for k in range(4)], axis=1
    )
    grad = dot_nn(within, high) + dot_nn(within, low)
    back = dot_nt(lhs[:split], high) + dot_nt(lhs[:split], low)
    gathered = back[:, 3 * rows :]
    for k in (2, 1, 0):
        gathered = jnp.where(sub < bounds[k + 1], back[:, k * rows : (k + 1) * rows], gathered)
    if split < feat:
        high3, low3 = high[3 * rows :], low[3 * rows :]
        grad_far = dot_nn(partner_t[split:], high3) + dot_nn(partner_t[split:], low3)
        grad = jnp.concatenate([grad, grad_far], axis=0)
        back_far = dot_nt(lhs[split:], high3) + dot_nt(lhs[split:], low3)
        gathered = jnp.concatenate([gathered, back_far], axis=0)
    rel_high, rel_low = split_bf(grad * left[...].astype(F32))
    half = send_out.shape[1]
    hot = rel_hot[pl.ds(pl.multiple_of((1 - core) * half, half), half), :]
    send_out[...] = (dot_nt(rel_high, hot) + dot_nt(rel_low, hot)).astype(send_out.dtype)
    hot = rel_hot[pl.ds(pl.multiple_of(core * half, half), half), :]
    keep_out[...] = dot_nt(rel_high, hot) + dot_nt(rel_low, hot)
    partner_out[...] = gathered.astype(BF16)
    left_high, left_low = split_bf(grad * rel_rows[...])
    hot = left_hot[...]
    own_out[...] = dot_nt(left_high, hot) + dot_nt(left_low, hot)


def chip_kernel(scal, keep, came, back, mine_out, *sends):
    step, piece = piece_rows(keep.shape[0])
    half = keep.shape[1]
    _, chip = place_of(scal)
    for s in range(4):
        span = pl.ds(pl.multiple_of((chip ^ s) * step, TILE), piece)
        total = keep[span, :] + came[span, :].astype(F32)
        if s == 0:
            mine_out[...] = total
        else:
            sends[s - 1][:, :half] = total.astype(BF16)
            sends[s - 1][:, half:] = back[span, :]


def plane_kernel(scal, mine, back, got1, got2, got3, sum_out, pack_out):
    half = mine.shape[1]
    step, piece = piece_rows(back.shape[0])
    _, chip = place_of(scal)
    total = mine[...]
    pack_out[0] = back[pl.ds(pl.multiple_of(chip * step, TILE), piece), :]
    for s, got in ((1, got1), (2, got2), (3, got3)):
        total = total + got[:, :half].astype(F32)
        pack_out[s] = got[:, half:]
    sum_out[...] = total.astype(BF16)


def route_kernel(scal, mine, layer1, layer2, layer3, pack, other, total_out, own_out, *sends, chips):
    half = mine.shape[1]
    core, chip = place_of(scal)
    total = (mine[...].astype(F32) + layer1[...].astype(F32)) + (
        layer2[...].astype(F32) + layer3[...].astype(F32)
    )
    total = total.astype(BF16)
    total_out[...] = total
    for s in range(4):
        target = 2 * (chip ^ s) + core
        source = jnp.int32(0)
        for number in range(2 * chips):
            source = jnp.where(scal[2 + number] == target, number, source)
        slot = (source >> 1) ^ chip
        routed = jnp.where((source & 1) == core, pack[slot], other[slot])
        if s == 0:
            own_out[...] = routed
        else:
            sends[s - 1][:, :half] = total
            sends[s - 1][:, half:] = routed


def adagrad_lanes(values, state, grad, values_out, state_out, span):
    mean = jnp.sum(grad * grad, axis=0, keepdims=True) * (1.0 / grad.shape[0])
    new_state = state[:, span] + mean
    state_out[:, span] = new_state
    scale = LEARN / (jnp.sqrt(new_state) + EPSILON)
    values_out[:, span] = values[:, span] - grad * scale


def finish_kernel(
    scal, rel, rel_state, ent, ent_state, own_grad, routed, mine0, mine1, mine2, mine3,
    peer0, peer1, peer2, peer3, ent_out, ent_state_out, rel_out, rel_state_out,
    mine_slots, peer_slots, ent_slots,
):
    feat = rel.shape[0]
    half = mine0.shape[1]
    step, piece = piece_rows(feat)
    core, chip = place_of(scal)
    for s, (mine, peer) in enumerate(((mine0, peer0), (mine1, peer1), (mine2, peer2), (mine3, peer3))):
        slot = chip ^ s
        mine_slots[slot] = mine[:, :half]
        peer_slots[slot] = peer[:, :half]
        ent_slots[slot] = routed[...] if s == 0 else mine[:, half:]
    sizes = (step, step, step, piece)

    def rows_of(slots):
        return jnp.concatenate([slots[j, : sizes[j], :] for j in range(4)], axis=0)

    grad = own_grad[...] + rows_of(ent_slots).astype(F32)
    adagrad_lanes(ent, ent_state, grad, ent_out, ent_state_out, slice(0, ent.shape[1]))
    mine, peer = rows_of(mine_slots), rows_of(peer_slots)
    for part in range(2):
        grad = jnp.where(core == part, mine, peer).astype(F32)
        adagrad_lanes(rel, rel_state, grad, rel_out, rel_state_out, slice(part * half, (part + 1) * half))


def near(value):
    return pltpu.with_memory_space_constraint(value, pltpu.VMEM)


def call(kernel, name, operands, outs, *, scalars=None, scratch=(), flops=0):
    specs = [pl.BlockSpec(memory_space=pltpu.VMEM) for _ in operands]
    operands = [near(value) for value in operands]
    if scalars is not None:
        specs = [pl.BlockSpec(memory_space=pltpu.SMEM)] + specs
        operands = [scalars] + operands
    shapes = [
        pltpu.VMEM(shape, dtype) if stays else jax.ShapeDtypeStruct(shape, dtype) for shape, dtype, stays in outs
    ]
    moved = sum(value.size * value.dtype.itemsize for value in operands)
    return pl.pallas_call(
        kernel,
        in_specs=specs,
        out_specs=[pl.BlockSpec(memory_space=pltpu.VMEM) for _ in outs],
        out_shape=shapes,
        scratch_shapes=list(scratch),
        compiler_params=pltpu.CompilerParams(vmem_limit_bytes=VMEM_BYTES),
        cost_estimate=pl.CostEstimate(flops=flops, bytes_accessed=moved, transcendentals=0),
        name=name,
    )(*operands)


def prepare(lhs_ids, rel_ids, negatives, own, relations):
    edges = lhs_ids.shape[1]
    feat, slice_rows = own.shape
    rel_total = relations.shape[1]
    outs = [
        ((feat, edges), BF16, True),
        ((feat, edges), F32, True),
        ((feat, edges), BF16, True),
        ((negatives.shape[0], slice_rows, BLOCK), F32, True),
        ((slice_rows, edges), BF16, True),
        ((rel_total, edges), BF16, True),
    ]
    flops = 4 * feat * edges * rel_total
    return call(prep_kernel, "prep", [lhs_ids, rel_ids, negatives, own, relations], outs, flops=flops)


def train(scalars, rhs_ids, prepared, candidates, neg_total, send_type):
    feat, edges = prepared[0].shape
    rows = candidates[0].shape[1]
    half = prepared[5].shape[0] // 2
    outs = [
        ((feat, rows), F32, True),
        ((feat, rows), BF16, True),
        ((feat, half), F32, True),
        ((feat, half), send_type, True),
    ]
    kernel = functools.partial(train_kernel, neg_total=neg_total, candidates=len(candidates))
    return call(
        kernel, "train", [rhs_ids, *prepared, *candidates], outs, scalars=scalars, flops=8 * feat * edges * half
    )


def adagrad(values, state, gradient):
    new_state = state + jnp.mean(gradient * gradient, axis=0)
    return values - LEARN * gradient / (jnp.sqrt(new_state) + EPSILON), new_state


def route_slices(value, order):
    peer_count = lax.axis_size("dom")
    feat, rows = value.shape
    pieces = value.T.reshape(peer_count, rows // peer_count, feat)
    spread = lax.all_to_all(pieces, "dom", split_axis=0, concat_axis=0, tiled=True)
    ordered = jnp.take(spread, order, axis=0)
    arrived = lax.all_to_all(ordered, "dom", split_axis=0, concat_axis=0, tiled=True)
    return arrived.reshape(rows, feat).T


def invert(matching):
    positions = jnp.arange(matching.shape[0], dtype=jnp.int32)
    return jnp.sum(jnp.where(matching[None, :] == positions[:, None], positions[None, :], 0), axis=1)


def wide_step(own, ent_state, relations, rel_state, lhs_ids, rhs_ids, rel_ids, negatives, matching, live):
    partner = route_slices(own.astype(BF16), matching)
    prepared = prepare(lhs_ids, rel_ids, negatives, own, relations)
    scalars = jnp.concatenate([jnp.zeros((1,), jnp.int32), live])
    grad_own, grad_partner, keep, send = train(scalars, rhs_ids, prepared, [partner], negatives.shape[1], F32)
    returned = route_slices(grad_partner, invert(matching)).astype(F32)
    new_rows, new_row_state = adagrad(own, ent_state[0], grad_own + returned)
    total = lax.psum(jnp.concatenate([keep, send], axis=1), ("dom", "rep"))
    new_relations, new_rel_state = adagrad(relations, rel_state[0], total)
    return new_rows, new_row_state[None], new_relations, new_rel_state[None]


def swap(value, axis, shift):
    size = lax.axis_size(axis)
    return lax.ppermute(value, axis, [(i, i ^ shift) for i in range(size)])


def near_step(own, ent_state, relations, rel_state, lhs_ids, rhs_ids, rel_ids, negatives, matching, live):
    feat, rel_total = relations.shape
    rows = own.shape[1]
    half = rel_total // 2
    step, piece = piece_rows(feat)
    place = lax.axis_index("dom")
    scalars = jnp.concatenate([place[None].astype(jnp.int32), live, matching])

    own_bf = own.astype(BF16)
    slices = [own_bf] + [swap(own_bf, "dom", 2 * s) for s in (1, 2, 3)]
    prepared = prepare(lhs_ids, rel_ids, negatives, own, relations)
    choice = (matching[place ^ 1] >> 1) ^ (place >> 1)
    wanted = slices[0]
    for s in (1, 2, 3):
        wanted = jnp.where(choice == s, slices[s], wanted)
    crossed = swap(wanted, "dom", 1)
    grad_own, grad_partner, keep, send = train(
        scalars, rhs_ids, prepared, slices + [crossed], negatives.shape[1], BF16
    )
    came = swap(send, "dom", 1)
    packed = ((piece, half + rows), BF16, True)
    mine, *sends = call(
        chip_kernel, "chip", [keep, came, grad_partner], [((piece, half), F32, True)] + [packed] * 3, scalars=scalars
    )
    got = [swap(sends[s - 1], "dom", 2 * s) for s in (1, 2, 3)]
    plane, pack = call(
        plane_kernel, "plane", [mine, grad_partner, *got],
        [((piece, half), BF16, True), ((4, piece, rows), BF16, True)], scalars=scalars,
    )
    layers = [swap(plane, "rep", s) for s in (1, 2, 3)]
    other = swap(pack, "dom", 1)
    total, routed, *sends = call(
        functools.partial(route_kernel, chips=4), "route", [plane, *layers, pack, other],
        [((piece, half), BF16, True), ((piece, rows), BF16, True)] + [packed] * 3, scalars=scalars,
    )
    peer_total = swap(total, "dom", 1)
    got = [swap(sends[s - 1], "dom", 2 * s) for s in (1, 2, 3)]
    peers = [swap(value, "dom", 1) for value in got]
    return call(
        finish_kernel, "finish",
        [relations, rel_state, own, ent_state, grad_own, routed, total, *got, peer_total, *peers],
        [((feat, rows), F32, False), ((1, rows), F32, False), ((feat, rel_total), F32, False), ((1, rel_total), F32, False)],
        scalars=scalars,
        scratch=[pltpu.VMEM((4, piece, half), BF16), pltpu.VMEM((4, piece, half), BF16), pltpu.VMEM((4, piece, rows), BF16)],
    )


def shards(
    entities,
    entity_state,
    relations,
    relation_state,
    lhs_rows,
    rhs_rows,
    relation_ids,
    neg_rows,
    matching,
    edge_counts,
):
    small = lax.axis_size("dom") == 8 and lax.axis_size("rep") == 4
    step = near_step if small else wide_step
    new_rows, new_row_state, new_relations, new_rel_state = step(
        entities[0].T, entity_state, relations.T, relation_state[None], lhs_rows, rhs_rows, relation_ids,
        neg_rows[0], matching, edge_counts[0],
    )
    return (new_rows.T[None], new_row_state, new_relations.T, new_rel_state[0])


def solution(mesh):
    return jax.shard_map(
        shards,
        mesh=mesh,
        in_specs=(
            P("dom", "rep", None),
            P("dom", "rep"),
            P(),
            P(),
            P("dom", "rep"),
            P("dom", "rep"),
            P("dom", "rep"),
            P("dom", "rep", None),
            P(),
            P("dom", "rep"),
        ),
        out_specs=(P("dom", "rep", None), P("dom", "rep"), P(), P()),
        check_vma=False,
    )
```

```python
import functools

import jax
import jax.numpy as jnp
from jax import lax
from jax.experimental import pallas as pl
from jax.experimental.pallas import tpu as pltpu
from jax.sharding import PartitionSpec as P

BLOCK = 128
TILE = 16
LEARN = 0.1
EPSILON = 1e-06
F32 = jnp.float32
BF16 = jnp.bfloat16
VMEM_BYTES = 24 * 1024 * 1024


def segment_bounds(feat_width):
    return (0, feat_width // 8, feat_width // 4, feat_width // 2, feat_width)


def tile_up(value, tile):
    return -(-value // tile) * tile


def split_bf(value):
    high = value.astype(BF16)
    return high, (value - high.astype(F32)).astype(BF16)


def dot_nn(a, b):
    return lax.dot_general(a, b, (((1,), (0,)), ((), ())), preferred_element_type=F32)


def dot_nt(a, b):
    return lax.dot_general(a, b, (((1,), (1,)), ((), ())), preferred_element_type=F32)


def one_hot(ids_row, count):
    rows = lax.broadcasted_iota(jnp.int32, (count, ids_row.shape[1]), 0)
    return jnp.where(rows == ids_row, 1.0, 0.0).astype(BF16)


def prep_kernel(
    lhs_hbm, rel_ids_hbm, neg_hbm, own_hbm, rel_hbm, matching_hbm,
    left_out, relrow_out, lhs_out, count_out, left_hot, rel_hot, choice_out, order_out,
    lhs_ids, rel_ids, negatives, own, rel, matching, sems, *, chips,
):
    pairs = ((rel_ids_hbm, rel_ids), (rel_hbm, rel), (lhs_hbm, lhs_ids), (own_hbm, own), (neg_hbm, negatives))
    copies = [pltpu.make_async_copy(source, target, sems.at[i]) for i, (source, target) in enumerate(pairs)]
    if chips:
        copies.append(pltpu.make_async_copy(matching_hbm, matching, sems.at[len(pairs)]))
    for copy in copies:
        copy.start()
    slice_rows = own.shape[1]
    copies[0].wait()
    hot = one_hot(rel_ids[...], rel.shape[1])
    rel_hot[...] = hot
    copies[1].wait()
    rel_high, rel_low = split_bf(rel[...])
    rel_rows = dot_nn(rel_high, hot) + dot_nn(rel_low, hot)
    relrow_out[...] = rel_rows
    copies[2].wait()
    copies[3].wait()
    hot = one_hot(lhs_ids[...], slice_rows)
    left_hot[...] = hot
    left = dot_nn(own[...].astype(BF16), hot)
    left_out[...] = left.astype(BF16)
    lhs_out[...] = (left * rel_rows).astype(BF16)
    copies[4].wait()
    ones = jnp.ones((BLOCK, negatives.shape[1]), BF16)
    for block in range(negatives.shape[0]):
        count_out[block] = dot_nt(one_hot(negatives[block : block + 1, :], slice_rows), ones)
    if chips:
        copies[5].wait()
        core, chip = place_of()

        def slot_of(source):
            return ((source >> 1) ^ chip) + jnp.where((source & 1) == core, 0, chips)

        choice_out[0] = jnp.full(choice_out.shape[1:], (matching[2 * chip + 1 - core] >> 1) ^ chip, jnp.int32)
        choice_out[1] = jnp.full(choice_out.shape[1:], slot_of(matching[2 * chip + core]), jnp.int32)
        for s in range(chips):
            target = 2 * (chip ^ s) + core
            source = jnp.int32(0)
            for number in range(2 * chips):
                source = jnp.where(matching[number] == target, number, source)
            order_out[s] = jnp.full(order_out.shape[1:], slot_of(source), jnp.int32)


def place_of():
    place = lax.axis_index("dom")
    return place & 1, place >> 1


def train_kernel(*refs, neg_total, candidates):
    counts_of, choice, rhs_ids, left, rel_rows, lhs_ref, counts, left_hot, rel_hot = refs[:9]
    near = refs[9 : 9 + candidates]
    own_out, partner_out, keep_out, send_out = refs[9 + candidates :]
    feat, edges = lhs_ref.shape
    rows = near[0].shape[1]
    blocks = edges // BLOCK
    bounds = segment_bounds(feat)
    split = min(feat, tile_up(bounds[3], TILE))
    deep = min(feat, tile_up(bounds[3], 256))
    live = counts_of[0, 0]
    core = place_of()[0] if candidates > 1 else 0
    wanted = choice[1]
    partner_f = near[-1][...].astype(F32)
    for number in range(candidates - 1):
        partner_f = jnp.where(wanted == number, near[number][...].astype(F32), partner_f)
    partner_t = partner_f.astype(BF16)
    zero = jnp.zeros((), BF16)
    partner = jnp.transpose(partner_f).astype(BF16)
    lane = lax.broadcasted_iota(jnp.int32, (rows, deep), 1)
    prefix = jnp.concatenate(
        [jnp.where(lane < bounds[k + 1], partner[:, :deep], zero) for k in range(3)], axis=0
    )
    lhs = lhs_ref[...]
    scores_low = dot_nn(prefix, lhs[:deep])
    scores_all = dot_nn(partner, lhs)
    row_iota = lax.broadcasted_iota(jnp.int32, (rows, BLOCK), 0)
    edge_iota = lax.broadcasted_iota(jnp.int32, (rows, BLOCK), 1)
    high_parts = [[], [], [], []]
    low_parts = [[], [], [], []]
    for block in range(blocks):
        span = slice(block * BLOCK, (block + 1) * BLOCK)
        alive = (edge_iota + block * BLOCK) < live
        weight = jnp.where(alive, counts[block] * (1.0 / neg_total), 0.0)
        hit = (row_iota == rhs_ids[:, span]) & alive
        run = None
        for k in (3, 2, 1, 0):
            score = scores_all[:, span] if k == 3 else scores_low[k * rows : (k + 1) * rows, span]
            tail = jnp.exp(-jnp.abs(score))
            big = 1.0 / (1.0 + tail)
            small = tail * big
            up = score >= 0.0
            coef = weight * jnp.where(up, big, small) - jnp.where(hit, jnp.where(up, small, big), 0.0)
            run = coef if run is None else run + coef
            high, low = split_bf(run)
            high_parts[k].append(high)
            low_parts[k].append(low)
    high = jnp.concatenate([jnp.concatenate(p, axis=1) for p in high_parts], axis=0)
    low = jnp.concatenate([jnp.concatenate(p, axis=1) for p in low_parts], axis=0)
    sub = lax.broadcasted_iota(jnp.int32, (split, rows), 0)
    within = jnp.concatenate(
        [jnp.where((sub >= bounds[k]) & (sub < bounds[k + 1]), partner_t[:split], zero) for k in range(4)], axis=1
    )
    grad = dot_nn(within, high) + dot_nn(within, low)
    back = dot_nt(lhs[:split], high) + dot_nt(lhs[:split], low)
    gathered = back[:, 3 * rows :]
    for k in (2, 1, 0):
        gathered = jnp.where(sub < bounds[k + 1], back[:, k * rows : (k + 1) * rows], gathered)
    if split < feat:
        high3, low3 = high[3 * rows :], low[3 * rows :]
        grad_far = dot_nn(partner_t[split:], high3) + dot_nn(partner_t[split:], low3)
        grad = jnp.concatenate([grad, grad_far], axis=0)
        back_far = dot_nt(lhs[split:], high3) + dot_nt(lhs[split:], low3)
        gathered = jnp.concatenate([gathered, back_far], axis=0)
    rel_high, rel_low = split_bf(grad * left[...].astype(F32))
    half = send_out.shape[1]
    hot = rel_hot[pl.ds(pl.multiple_of((1 - core) * half, half), half), :]
    send_out[...] = (dot_nt(rel_high, hot) + dot_nt(rel_low, hot)).astype(send_out.dtype)
    hot = rel_hot[pl.ds(pl.multiple_of(core * half, half), half), :]
    keep_out[...] = dot_nt(rel_high, hot) + dot_nt(rel_low, hot)
    partner_out[...] = gathered.astype(BF16)
    left_high, left_low = split_bf(grad * rel_rows[...])
    hot = left_hot[...]
    own_out[...] = dot_nt(left_high, hot) + dot_nt(left_low, hot)


def parcel_step(feat_width):
    return (feat_width // 4) // TILE * TILE


def fits_parcels(feat_width, half, rows):
    return half == 3 * BLOCK and rows == BLOCK and feat_width - 4 * parcel_step(feat_width) == TILE


def chip_kernel(keep, came, back, mine_out, mine_ent, *outs):
    sends, spare = outs[:3], outs[3]
    feat, half = keep.shape
    step = parcel_step(feat)
    tiles = half // BLOCK
    _, chip = place_of()
    last = slice(4 * step, feat)
    for t in range(tiles):
        lanes = slice(t * BLOCK, (t + 1) * BLOCK)
        spare[t] = keep[last, lanes] + came[last, lanes].astype(F32)
    spare[tiles] = back[last, :].astype(F32)
    for s in range(4):
        span = pl.ds(pl.multiple_of((chip ^ s) * step, TILE), step)
        total = keep[span, :] + came[span, :].astype(F32)
        rest = spare[chip ^ s]
        for t in range(tiles):
            part = total[:, t * BLOCK : (t + 1) * BLOCK]
            if s == 0:
                mine_out[t * step : (t + 1) * step, :] = part
            else:
                sends[s - 1][t * step : (t + 1) * step, :] = part.astype(BF16)
        if s == 0:
            mine_out[tiles * step :, :] = rest
            mine_ent[:step, :] = back[span, :]
            mine_ent[step:, :] = rest.astype(BF16)
        else:
            sends[s - 1][tiles * step : 4 * step, :] = back[span, :]
            sends[s - 1][4 * step :, :] = rest.astype(BF16)


def plane_kernel(mine, mine_ent, got1, got2, got3, sum_out, pack_out):
    step = pack_out.shape[1] - TILE
    body = 3 * step
    total = mine[:body, :]
    rest = mine[body:, :]
    pack_out[0] = mine_ent[...]
    for s, got in ((1, got1), (2, got2), (3, got3)):
        total = total + got[:body, :].astype(F32)
        rest = rest + got[4 * step :, :].astype(F32)
        pack_out[s] = got[body:, :]
    sum_out[:body, :] = total.astype(BF16)
    sum_out[body:, :] = rest.astype(BF16)


def route_kernel(mine, layer1, layer2, layer3, pack, other, order, total_out, own_out, *sends):
    step = pack.shape[1] - TILE
    body = 3 * step
    _, chip = place_of()
    total = (mine[...].astype(F32) + layer1[...].astype(F32)) + (
        layer2[...].astype(F32) + layer3[...].astype(F32)
    )
    total_out[...] = total.astype(BF16)
    held = [pack[s].astype(F32) for s in range(4)] + [other[s].astype(F32) for s in range(4)]
    for s in range(4):
        slot = order[s]
        routed = held[-1]
        for number in range(len(held) - 1):
            routed = jnp.where(slot == number, held[number], routed)
        if s == 0:
            own_out[...] = routed
        else:
            sends[s - 1][:body, :] = total[:body, :].astype(BF16)
            sends[s - 1][body : 4 * step, :] = routed[:step, :].astype(BF16)
            rest = jnp.where(chip == 3, routed[step:, :], total[body:, :])
            sends[s - 1][4 * step :, :] = rest.astype(BF16)


def adagrad_lanes(values, state, grad):
    mean = jnp.sum(grad * grad, axis=0, keepdims=True) * (1.0 / grad.shape[0])
    new_state = state + mean
    return values - grad * (LEARN / (jnp.sqrt(new_state) + EPSILON)), new_state


def tile_rows(slots, tile, step):
    parts = [slots[j, tile * step : (tile + 1) * step, :] for j in range(4)]
    return jnp.concatenate(parts + [slots[tile, 4 * step :, :]], axis=0).astype(F32)


def half_update(core_half, slots, rel, state, new_values, new_state):
    feat, half = new_values.shape
    step = parcel_step(feat)
    for t in range(half // BLOCK):
        lanes = slice(t * BLOCK, (t + 1) * BLOCK)
        right = slice(half + t * BLOCK, half + (t + 1) * BLOCK)
        upper = core_half == 1
        values = jnp.where(upper, rel[:, right], rel[:, lanes])
        old = jnp.where(upper, state[:, right], state[:, lanes])
        new_values[:, lanes], new_state[:, lanes] = adagrad_lanes(values, old, tile_rows(slots, t, step))


def own_kernel(
    rel, rel_state, ent, ent_state, own_grad, routed, total, got1, got2, got3,
    ent_out, ent_state_out, rel_out, half_state, slots, new_values, sem,
):
    feat = rel.shape[0]
    step = parcel_step(feat)
    body = 3 * step
    core, chip = place_of()
    slots[chip, :body, :] = total[:body, :]
    slots[chip, body : 4 * step, :] = routed[:step, :].astype(BF16)
    rest = jnp.where(chip == 3, routed[step:, :], total[body:, :].astype(F32))
    slots[chip, 4 * step :, :] = rest.astype(BF16)
    for s, got in ((1, got1), (2, got2), (3, got3)):
        slots[chip ^ s] = got[...]
    half = new_values.shape[1]
    half_update(core, slots, rel, rel_state, new_values, half_state)
    start = pl.multiple_of(core * half, BLOCK)
    copy = pltpu.make_async_copy(new_values, rel_out.at[:, pl.ds(start, half)], sem)
    copy.start()
    grad = own_grad[...] + tile_rows(slots, 3, step)
    ent_out[...], ent_state_out[...] = adagrad_lanes(ent[...], ent_state[...], grad)
    copy.wait()


def peer_kernel(
    rel, rel_state, half_state, peer0, peer1, peer2, peer3, started, rel_out, rel_state_out,
    slots, new_values, new_state, sem,
):
    step = parcel_step(rel.shape[0])
    body = 3 * step
    core, chip = place_of()
    slots[chip, :body, :] = peer0[:body, :]
    slots[chip, 4 * step :, :] = peer0[body:, :]
    for s, peer in ((1, peer1), (2, peer2), (3, peer3)):
        slots[chip ^ s] = peer[...]
    half = new_values.shape[1]
    half_update(1 - core, slots, rel, rel_state, new_values, new_state)
    start = pl.multiple_of((1 - core) * half, BLOCK)
    copy = pltpu.make_async_copy(new_values, rel_out.at[:, pl.ds(start, half)], sem)
    copy.start()
    mine, peer = half_state[...], new_state[...]
    rel_state_out[:half] = jnp.where(core == 0, mine, peer)[0]
    rel_state_out[half:] = jnp.where(core == 0, peer, mine)[0]
    copy.wait()


VMEM_SPEC = pl.BlockSpec(memory_space=pltpu.VMEM)
SMEM_SPEC = pl.BlockSpec(memory_space=pltpu.SMEM)
ANY_SPEC = pl.BlockSpec(memory_space=pl.ANY)


def call(kernel, name, operands, outs, *, scalars=(), raw=(), scratch=(), flops=0, aliases=None):
    operands = [pltpu.with_memory_space_constraint(value, pltpu.VMEM) for value in operands]
    raw = [pltpu.with_memory_space_constraint(value, pltpu.HBM) for value in raw]
    specs = [SMEM_SPEC] * len(scalars) + [VMEM_SPEC] * len(operands) + [ANY_SPEC] * len(raw)
    shapes = [
        pltpu.VMEM(shape, dtype) if where == "vmem" else jax.ShapeDtypeStruct(shape, dtype)
        for shape, dtype, where in outs
    ]
    moved = sum(value.size * value.dtype.itemsize for value in operands)
    return pl.pallas_call(
        kernel,
        in_specs=specs,
        out_specs=[ANY_SPEC if where == "raw" else VMEM_SPEC for _, _, where in outs],
        out_shape=shapes,
        scratch_shapes=list(scratch),
        input_output_aliases=aliases or {},
        compiler_params=pltpu.CompilerParams(vmem_limit_bytes=VMEM_BYTES),
        cost_estimate=pl.CostEstimate(flops=flops, bytes_accessed=moved, transcendentals=0),
        name=name,
    )(*scalars, *operands, *raw)


def prepare(matching, lhs_ids, rel_ids, negatives, own, relations, chips):
    edges = lhs_ids.shape[1]
    feat, slice_rows = own.shape
    rel_total = relations.shape[1]
    outs = [
        ((feat, edges), BF16, "vmem"),
        ((feat, edges), F32, "vmem"),
        ((feat, edges), BF16, "vmem"),
        ((negatives.shape[0], slice_rows, BLOCK), F32, "vmem"),
        ((slice_rows, edges), BF16, "vmem"),
        ((rel_total, edges), BF16, "vmem"),
        ((2, 1, slice_rows), jnp.int32, "vmem"),
        ((4, 1, slice_rows), jnp.int32, "vmem"),
    ]
    arrays = [lhs_ids, rel_ids, negatives, own, relations]
    scratch = [pltpu.VMEM(value.shape, value.dtype) for value in arrays]
    scratch += [pltpu.SMEM(matching.shape, jnp.int32), pltpu.SemaphoreType.DMA((6,))]
    return call(
        functools.partial(prep_kernel, chips=chips), "prep", [], outs, raw=arrays + [matching],
        scratch=scratch, flops=4 * feat * edges * rel_total,
    )


def train(live, rhs_ids, prepared, candidates, neg_total, send_type):
    feat, edges = prepared[0].shape
    rows = candidates[0].shape[1]
    half = prepared[5].shape[0] // 2
    outs = [
        ((feat, rows), F32, "vmem"),
        ((feat, rows), BF16, "vmem"),
        ((feat, half), F32, "vmem"),
        ((feat, half), send_type, "vmem"),
    ]
    kernel = functools.partial(train_kernel, neg_total=neg_total, candidates=len(candidates))
    return call(
        kernel, "train", [prepared[6], rhs_ids, *prepared[:6], *candidates], outs, scalars=[live],
        flops=8 * feat * edges * half,
    )


def adagrad(values, state, gradient):
    new_state = state + jnp.mean(gradient * gradient, axis=0)
    return values - LEARN * gradient / (jnp.sqrt(new_state) + EPSILON), new_state


def route_slices(value, order):
    peer_count = lax.axis_size("dom")
    feat, rows = value.shape
    pieces = value.T.reshape(peer_count, rows // peer_count, feat)
    spread = lax.all_to_all(pieces, "dom", split_axis=0, concat_axis=0, tiled=True)
    ordered = jnp.take(spread, order, axis=0)
    arrived = lax.all_to_all(ordered, "dom", split_axis=0, concat_axis=0, tiled=True)
    return arrived.reshape(rows, feat).T


def invert(matching):
    positions = jnp.arange(matching.shape[0], dtype=jnp.int32)
    return jnp.sum(jnp.where(matching[None, :] == positions[:, None], positions[None, :], 0), axis=1)


def wide_step(own, ent_state, relations, rel_state, lhs_ids, rhs_ids, rel_ids, negatives, matching, live):
    partner = route_slices(own.astype(BF16), matching)
    prepared = prepare(matching, lhs_ids, rel_ids, negatives, own, relations, 0)
    grad_own, grad_partner, keep, send = train(live, rhs_ids, prepared, [partner], negatives.shape[1], F32)
    returned = route_slices(grad_partner, invert(matching)).astype(F32)
    new_rows, new_row_state = adagrad(own, ent_state[0], grad_own + returned)
    total = lax.psum(jnp.concatenate([keep, send], axis=1), ("dom", "rep"))
    new_relations, new_rel_state = adagrad(relations, rel_state[0], total)
    return new_rows, new_row_state[None], new_relations, new_rel_state


def swap(value, axis, shift):
    size = lax.axis_size(axis)
    return lax.ppermute(value, axis, [(i, i ^ shift) for i in range(size)])


def near_step(own, ent_state, relations, rel_state, lhs_ids, rhs_ids, rel_ids, negatives, matching, live):
    feat, rel_total = relations.shape
    rows = own.shape[1]
    half = rel_total // 2
    step = parcel_step(feat)
    summed = (3 * step + TILE, BLOCK)
    parcel = ((feat, BLOCK), BF16, "vmem")

    own_bf = own.astype(BF16)
    slices = [own_bf] + [swap(own_bf, "dom", 2 * s) for s in (1, 2, 3)]
    prepared = prepare(matching, lhs_ids, rel_ids, negatives, own, relations, 4)
    choice, order = prepared[6:]
    wanted = slices[0]
    for s in (1, 2, 3):
        wanted = jnp.where(choice[0] == s, slices[s], wanted)
    crossed = swap(wanted, "dom", 1)
    grad_own, grad_partner, keep, send = train(
        live, rhs_ids, prepared, slices + [crossed], negatives.shape[1], BF16
    )
    came = swap(send, "dom", 1)
    mine, mine_ent, *sends = call(
        chip_kernel, "chip", [keep, came, grad_partner],
        [(summed, F32, "vmem"), ((step + TILE, rows), BF16, "vmem")] + [parcel] * 3,
        scratch=[pltpu.VMEM((4, TILE, BLOCK), F32)],
    )
    got = [swap(sends[s - 1], "dom", 2 * s) for s in (1, 2, 3)]
    plane, pack = call(
        plane_kernel, "plane", [mine, mine_ent, *got],
        [(summed, BF16, "vmem"), ((4, step + TILE, rows), BF16, "vmem")],
    )
    layers = [swap(plane, "rep", s) for s in (1, 2, 3)]
    other = swap(pack, "dom", 1)
    total, routed, *sends = call(
        route_kernel, "route", [plane, *layers, pack, other, order],
        [(summed, BF16, "vmem"), ((step + TILE, rows), F32, "vmem")] + [parcel] * 3,
    )
    peer_total = swap(total, "dom", 1)
    got = [swap(sends[s - 1], "dom", 2 * s) for s in (1, 2, 3)]
    peers = [swap(value, "dom", 1) for value in got]
    scratch = [pltpu.VMEM((4, feat, BLOCK), BF16), pltpu.VMEM((feat, half), F32)]
    new_rows, new_row_state, started, half_state = call(
        own_kernel, "own", [relations, rel_state, own, ent_state, grad_own, routed, total, *got],
        [((feat, rows), F32, "hbm"), ((1, rows), F32, "hbm"), ((feat, rel_total), F32, "raw"), ((1, half), F32, "vmem")],
        scratch=scratch + [pltpu.SemaphoreType.DMA],
    )
    new_relations, new_rel_state = call(
        peer_kernel, "peer", [relations, rel_state, half_state, peer_total, *peers],
        [((feat, rel_total), F32, "raw"), ((rel_total,), F32, "hbm")],
        raw=[started], aliases={7: 0}, scratch=scratch + [pltpu.VMEM((1, half), F32), pltpu.SemaphoreType.DMA],
    )
    return new_rows, new_row_state, new_relations, new_rel_state


def shards(
    entities,
    entity_state,
    relations,
    relation_state,
    lhs_rows,
    rhs_rows,
    relation_ids,
    neg_rows,
    matching,
    edge_counts,
):
    small = lax.axis_size("dom") == 8 and lax.axis_size("rep") == 4
    small = small and fits_parcels(relations.shape[1], relations.shape[0] // 2, entities.shape[1])
    step = near_step if small else wide_step
    new_rows, new_row_state, new_relations, new_rel_state = step(
        entities[0].T, entity_state, relations.T, relation_state[None], lhs_rows, rhs_rows, relation_ids,
        neg_rows[0], matching, edge_counts,
    )
    return (new_rows.T[None], new_row_state, new_relations.T, new_rel_state)


def solution(mesh):
    return jax.shard_map(
        shards,
        mesh=mesh,
        in_specs=(
            P("dom", "rep", None),
            P("dom", "rep"),
            P(),
            P(),
            P("dom", "rep"),
            P("dom", "rep"),
            P("dom", "rep"),
            P("dom", "rep", None),
            P(),
            P("dom", "rep"),
        ),
        out_specs=(P("dom", "rep", None), P("dom", "rep"), P(), P()),
        check_vma=False,
    )
```
